32 devices in a mesh: ha: 8 (over z, core), gz: 4 (over y, x).
Axes of the slice: x: 2, y: 2, z: 4, core: 2. Of those that a mesh axis runs over, the one named last changes fastest.
Arguments:
- velocity: bfloat16 [16, 2048, 2048], P('gz', 'ha'), may hold values from -48 to 48
- lower_coef: float32 [16], P('gz'), may hold values from 200 to 20000
- upper_coef: float32 [16], P('gz'), may hold values from 200 to 20000
Outputs:
- diffused: bfloat16 [16, 2048, 2048], P('gz', 'ha')
The draws below stay inside these ranges and needn't reach their ends.
All inputs are finite; a program needn't handle non-finite values.
Results may differ from the reference program's by a relative error of at most 0.012.
The reference program's roundings to bfloat16 on the way count: a program that leaves them out, or rounds other values in their place, can miss the bound.
Values may be sent and summed in bfloat16 or wider, within the bound.
A program may use at most 64 MiB of HBM per device.

```python
import math
import jax
import jax.numpy as jnp
from jax import lax

NX = 2048
NY = 2048
KYW = 128
NZ = 16


def draw_velocity(key, part):
    white_key = jax.random.fold_in(key, 0)
    noise_part = jax.random.normal(white_key, (NZ, NX, NY), jnp.float32)
    grid_field = 8.0 * noise_part
    return jnp.clip(grid_field, -48.0, 48.0).astype(jnp.bfloat16)


def draw_lower_coef(key, part):
    sub_key = jax.random.fold_in(key, 11)
    upper_end = 20000.0
    uniform_part = jax.random.uniform(sub_key, (NZ,), jnp.float32)
    values = 200.0 * jnp.exp(uniform_part * jnp.log(jnp.float32(upper_end / 200.0)))
    return jnp.clip(values, 200.0, 20000.0).astype(jnp.float32)


def draw_upper_coef(key, part):
    sub_key = jax.random.fold_in(key, 23)
    upper_end = 20000.0
    uniform_part = jax.random.uniform(sub_key, (NZ,), jnp.float32)
    values = 200.0 * jnp.exp(uniform_part * jnp.log(jnp.float32(upper_end / 200.0)))
    return jnp.clip(values, 200.0, 20000.0).astype(jnp.float32)


def setup_inputs(seed: int = 0) -> dict:
    arg_keys = jax.random.split(jax.random.key(seed), 4)
    return {
        "velocity": draw_velocity(jax.random.fold_in(arg_keys[3], 71), 0),
        "lower_coef": draw_lower_coef(jax.random.fold_in(arg_keys[3], 71), 0),
        "upper_coef": draw_upper_coef(jax.random.fold_in(arg_keys[3], 71), 0),
    }


wavenumber_scale = 0.001

def tables(length, mode_count):
    position = jnp.arange(length, dtype=jnp.int32)[:, None]
    wave_index = jnp.arange(mode_count, dtype=jnp.int32)[None, :]
    angles = (position * wave_index % length).astype(jnp.float32) * (2.0 * math.pi / length)
    factor = 1.0 / math.sqrt(length)
    return ((jnp.cos(angles) * factor).astype(jnp.bfloat16), (jnp.sin(angles) * factor).astype(jnp.bfloat16))

def thomas(lower_band, main_band, upper_band, source):

    def forward(running, packed):
        upper_prev, previous_source = running
        lower_row, main_row, upper_row, source_row = packed
        inverse = 1.0 / (main_row - lower_row * upper_prev)
        upper_new = upper_row * inverse
        source_new = (source_row - lower_row[None] * previous_source) * inverse[None]
        return ((upper_new, source_new), (upper_new, source_new))
    initial = (jnp.zeros_like(main_band[0]), jnp.zeros_like(source[0]))
    unused, (upper_mod, source_mod) = lax.scan(forward, initial, (lower_band, main_band, upper_band, source))

    def backward(running, packed):
        upper_row, source_row = packed
        result = source_row - upper_row[None] * running
        return (result, result)
    unused, solved = lax.scan(backward, jnp.zeros_like(source[0]), (upper_mod, source_mod), reverse=True)
    return solved

def reference(velocity, lower_coef, upper_coef):
    y_cosine, y_sine = tables(NY, KYW)
    x_cosine, x_sine = tables(NX, NX)
    flattened = velocity.reshape(NZ * NX, NY)
    spec_re = jnp.dot(flattened, y_cosine, preferred_element_type=jnp.float32).astype(jnp.bfloat16)
    spec_im = (-jnp.dot(flattened, y_sine, preferred_element_type=jnp.float32)).astype(jnp.bfloat16)
    spec_re, spec_im = lax.optimization_barrier((spec_re, spec_im))
    real_in = spec_re.astype(jnp.float32).reshape(NZ, NX, KYW)
    imag_in = spec_im.astype(jnp.float32).reshape(NZ, NX, KYW)
    cos_full = x_cosine.astype(jnp.float32)
    sin_full = x_sine.astype(jnp.float32)
    wave_re = jnp.einsum('zxq,xp->zpq', real_in, cos_full) + jnp.einsum('zxq,xp->zpq', imag_in, sin_full)
    wave_im = jnp.einsum('zxq,xp->zpq', imag_in, cos_full) - jnp.einsum('zxq,xp->zpq', real_in, sin_full)
    kx_index = jnp.arange(NX, dtype=jnp.int32)
    streamwise_signed_wave = jnp.where(kx_index < NX // 2, kx_index, kx_index - NX).astype(jnp.float32)
    spanwise_wave_value = jnp.arange(KYW, dtype=jnp.int32).astype(jnp.float32)
    viscous_decay = 1.0 + wavenumber_scale * (streamwise_signed_wave[:, None] * streamwise_signed_wave[:, None] + spanwise_wave_value[None, :] * spanwise_wave_value[None, :])
    main_band = viscous_decay[None] + (lower_coef + upper_coef)[:, None, None]
    zindex = jnp.arange(NZ, dtype=jnp.int32)
    sub_coef = jnp.where(zindex == 0, jnp.zeros_like(lower_coef), -lower_coef)
    sup_coef = jnp.where(zindex == NZ - 1, jnp.zeros_like(upper_coef), -upper_coef)
    lower_band = jnp.broadcast_to(sub_coef[:, None, None], main_band.shape)
    upper_band = jnp.broadcast_to(sup_coef[:, None, None], main_band.shape)
    source = jnp.stack([wave_re, wave_im], 1)
    solved = thomas(lower_band, main_band, upper_band, source)
    rounded = lax.optimization_barrier(solved.astype(jnp.bfloat16)).astype(jnp.float32)
    sol_re = rounded[:, 0]
    sol_im = rounded[:, 1]
    back_re = (jnp.einsum('zpq,px->zxq', sol_re, cos_full) - jnp.einsum('zpq,px->zxq', sol_im, sin_full)).astype(jnp.bfloat16)
    back_im = (jnp.einsum('zpq,px->zxq', sol_im, cos_full) + jnp.einsum('zpq,px->zxq', sol_re, sin_full)).astype(jnp.bfloat16)
    weight = jnp.where(jnp.arange(KYW, dtype=jnp.int32) == 0, 1.0, 2.0).astype(jnp.float32)
    w_cosine = (y_cosine.astype(jnp.float32) * weight[None, :]).astype(jnp.bfloat16)
    w_sine = (y_sine.astype(jnp.float32) * weight[None, :]).astype(jnp.bfloat16)
    result = jnp.dot(back_re.reshape(NZ * NX, KYW), w_cosine.T, preferred_element_type=jnp.float32)
    result = result - jnp.dot(back_im.reshape(NZ * NX, KYW), w_sine.T, preferred_element_type=jnp.float32)
    return result.astype(jnp.bfloat16).reshape(NZ, NX, NY)
```

```python
import functools
import math

import jax
import jax.numpy as jnp
import numpy as np
from jax import lax
from jax.experimental import pallas as pl
from jax.experimental.pallas import tpu as pltpu
from jax.sharding import PartitionSpec as P

NX = 2048
NY = 2048
KYW = 128
GROUP = 8
LANES = 128


wavenumber_scale = 0.001


def tables(length, mode_count):
    position = jnp.arange(length, dtype=jnp.int32)[:, None]
    wave_index = jnp.arange(mode_count, dtype=jnp.int32)[None, :]
    angles = (position * wave_index % length).astype(jnp.float32) * (2.0 * math.pi / length)
    factor = 1.0 / math.sqrt(length)
    return (
        (jnp.cos(angles) * factor).astype(jnp.bfloat16),
        (jnp.sin(angles) * factor).astype(jnp.bfloat16),
    )


def signed_wave(lane_index):
    return jnp.where(lane_index < NX // 2, lane_index, lane_index - NX).astype(jnp.float32)


def damping_for(kx_value, spanwise_wave_value):
    return 1.0 + wavenumber_scale * (
        kx_value[None, :] * kx_value[None, :]
        + spanwise_wave_value[:, None] * spanwise_wave_value[:, None]
    )


def band_pair(lower_coef, upper_coef, z_global, z_total):
    sub_coef = jnp.where(z_global == 0, jnp.zeros_like(lower_coef), -lower_coef)
    sup_coef = jnp.where(z_global == z_total - 1, jnp.zeros_like(upper_coef), -upper_coef)
    return (sub_coef, sup_coef)


def thomas(lower_band, main_band, upper_band, source):

    def forward(running, packed):
        upper_prev, previous_source = running
        lower_row, main_row, upper_row, source_row = packed
        inverse = 1.0 / (main_row - lower_row * upper_prev)
        upper_new = upper_row * inverse
        source_new = (source_row - lower_row[None] * previous_source) * inverse[None]
        return ((upper_new, source_new), (upper_new, source_new))

    initial = (jnp.zeros_like(main_band[0]), jnp.zeros_like(source[0]))
    unused, (upper_mod, source_mod) = lax.scan(
        forward, initial, (lower_band, main_band, upper_band, source)
    )

    def backward(running, packed):
        upper_row, source_row = packed
        result = source_row - upper_row[None] * running
        return (result, result)

    unused, solved = lax.scan(
        backward, jnp.zeros_like(source[0]), (upper_mod, source_mod), reverse=True
    )
    return solved


def body_general(velocity, lower_coef, upper_coef):
    depth_rows = velocity.shape[0]
    z_groups = lax.axis_size("gz")
    z_total = depth_rows * z_groups
    wave_count = KYW // lax.axis_size("ha")
    y_cosine, y_sine = tables(NY, KYW)
    x_cosine, x_sine = tables(NX, NX)
    spec_re = jnp.einsum("zxy,yk->zkx", velocity, y_cosine, preferred_element_type=jnp.float32)
    spec_im = -jnp.einsum("zxy,yk->zkx", velocity, y_sine, preferred_element_type=jnp.float32)
    spectrum = jnp.stack([spec_re, spec_im], 1).astype(jnp.bfloat16)
    block = lax.all_to_all(spectrum, "ha", split_axis=2, concat_axis=3, tiled=True)
    with_cos = jnp.dot(block, x_cosine, preferred_element_type=jnp.float32)
    with_sin = jnp.dot(block, x_sine, preferred_element_type=jnp.float32)
    source = jnp.stack([with_cos[:, 0] + with_sin[:, 1], with_cos[:, 1] - with_sin[:, 0]], 1)
    spanwise_wave_value = (
        lax.axis_index("ha") * wave_count + jnp.arange(wave_count, dtype=jnp.int32)
    ).astype(jnp.float32)
    lower_all, upper_all = (
        lax.all_gather(lower_coef, "gz", axis=0, tiled=True),
        lax.all_gather(upper_coef, "gz", axis=0, tiled=True),
    )
    columns = lax.all_to_all(source, "gz", split_axis=3, concat_axis=0, tiled=True)
    lane_count = NX // z_groups
    lane_index = lax.axis_index("gz") * lane_count + jnp.arange(lane_count, dtype=jnp.int32)
    z_every = jnp.arange(z_total, dtype=jnp.int32)
    sub_coef, sup_coef = band_pair(lower_all, upper_all, z_every, z_total)
    main_band = (
        damping_for(signed_wave(lane_index), spanwise_wave_value)[None]
        + (lower_all + upper_all)[:, None, None]
    )
    sub_band = jnp.broadcast_to(sub_coef[:, None, None], main_band.shape)
    sup_band = jnp.broadcast_to(sup_coef[:, None, None], main_band.shape)
    solved_columns = thomas(sub_band, main_band, sup_band, columns)
    solved = lax.all_to_all(
        solved_columns.astype(jnp.bfloat16), "gz", split_axis=0, concat_axis=3, tiled=True
    ).astype(solved_columns.dtype)
    rounded = solved.astype(jnp.bfloat16)
    part_cos = jnp.dot(rounded, x_cosine, preferred_element_type=jnp.float32)
    part_sin = jnp.dot(rounded, x_sine, preferred_element_type=jnp.float32)
    planes = jnp.stack(
        [part_cos[:, 0] - part_sin[:, 1], part_cos[:, 1] + part_sin[:, 0]], 1
    ).astype(jnp.bfloat16)
    weight = jnp.where(jnp.arange(KYW, dtype=jnp.int32) == 0, 1.0, 2.0).astype(jnp.float32)
    w_cosine = (y_cosine.astype(jnp.float32) * weight[None, :]).astype(jnp.bfloat16)
    w_sine = (y_sine.astype(jnp.float32) * weight[None, :]).astype(jnp.bfloat16)
    block = lax.all_to_all(planes, "ha", split_axis=3, concat_axis=2, tiled=True)
    result = jnp.einsum("nkx,yk->nxy", block[:, 0], w_cosine, preferred_element_type=jnp.float32)
    result = result - jnp.einsum(
        "nkx,yk->nxy", block[:, 1], w_sine, preferred_element_type=jnp.float32
    )
    return result.astype(jnp.bfloat16)


def host_tables(length, mode_count):
    position = np.arange(length)[:, None]
    wave_index = np.arange(mode_count)[None, :]
    angles = (position * wave_index % length) * (2.0 * math.pi / length)
    factor = 1.0 / math.sqrt(length)
    return np.cos(angles) * factor, np.sin(angles) * factor


def real_x_table():
    cosine, sine = host_tables(NX, NX // 2 + 1)
    half = NX // 2
    table = np.concatenate([cosine[:, :half], sine[:, :half]], 1)
    table[:, half] = cosine[:, half]
    return jnp.asarray(table, jnp.bfloat16)


def other_half_first(position, step, count):
    half = count // 2
    side = position // half
    base = jnp.where(step < half, (1 - side) * half, side * half)
    return base + (position + 1 + step) % half


def own_half_first(position, step, count):
    half = count // 2
    side = position // half
    base = jnp.where(step < half, side * half, (1 - side) * half)
    return base + (position + step) % half


def middle_kernel(
    n_ha, n_gz, depth,
    velocity_ref, y_table_ref, x_table_ref, lower_ref, upper_ref,
    out_ref,
    velocity, y_table, x_table, send1, recv1, wave, inverse, upper_mod, solved,
    send2, recv2, coef, coefs,
    load_sem, table_sem, own_sem,
    send1_sem, recv1_sem, send2_sem, recv2_sem, coef_send_sem, coef_recv_sem,
):
    ha = lax.axis_index("ha")
    gz = lax.axis_index("gz")
    count = n_ha * n_gz
    me = ha * n_gz + gz
    rows = velocity.shape[1]
    z_total = depth * n_gz
    block_rows = depth * GROUP
    bulk = z_total * GROUP
    half_ha = n_ha // 2
    half_channels = half_ha * n_gz * GROUP

    y_load = pltpu.make_async_copy(y_table_ref, y_table, load_sem.at[depth])
    y_load.start()
    loads = []
    for z in range(depth):
        load = pltpu.make_async_copy(velocity_ref.at[z], velocity.at[z], load_sem.at[z])
        load.start()
        loads.append(load)
    x_load = pltpu.make_async_copy(x_table_ref, x_table, table_sem)
    x_load.start()

    barrier = pltpu.get_barrier_semaphore()

    @pl.loop(1, count)
    def _(step):
        peer = (me + step) % count
        pl.semaphore_signal(
            barrier, inc=1, device_id={"ha": peer // n_gz, "gz": peer % n_gz},
            device_id_type=pl.DeviceIdType.MESH,
        )

    for z in range(depth):
        coef[pl.ds(z, 1), :] = jnp.full((1, LANES), lower_ref[z], jnp.float32)
        coef[pl.ds(depth + z, 1), :] = jnp.full((1, LANES), upper_ref[z], jnp.float32)

    def first_copy(h, g, slot_h, slot_g):
        return pltpu.make_async_remote_copy(
            src_ref=send1.at[h, g],
            dst_ref=recv1.at[slot_h, slot_g],
            send_sem=send1_sem.at[h * n_gz + g],
            recv_sem=recv1_sem.at[slot_h * n_gz + slot_g],
            device_id={"ha": h, "gz": g},
            device_id_type=pl.DeviceIdType.MESH,
        )

    def second_copy(h, g, slot):
        return pltpu.make_async_remote_copy(
            src_ref=send2.at[h, g],
            dst_ref=recv2.at[slot],
            send_sem=send2_sem.at[h * n_gz + g],
            recv_sem=recv2_sem.at[slot],
            device_id={"ha": h, "gz": g},
            device_id_type=pl.DeviceIdType.MESH,
        )

    def coef_copy(g, slot):
        return pltpu.make_async_remote_copy(
            src_ref=coef,
            dst_ref=coefs.at[slot],
            send_sem=coef_send_sem.at[g],
            recv_sem=coef_recv_sem.at[slot],
            device_id={"ha": ha, "gz": g},
            device_id_type=pl.DeviceIdType.MESH,
        )

    y_load.wait()
    for part in range(2):
        side = (ha // half_ha + 1 + part) % 2
        first = pl.multiple_of(side * half_channels, half_channels)
        planes = []
        for z in range(depth):
            if part == 0:
                loads[z].wait()
            planes.append(
                lax.dot_general(
                    y_table[pl.ds(first, half_channels), :], velocity[z],
                    (((1,), (1,)), ((), ())), preferred_element_type=jnp.float32,
                ).reshape(half_ha, n_gz, 1, GROUP, rows)
            )
        spectrum = jnp.concatenate(planes, 2).reshape(half_ha, n_gz, block_rows, rows)
        send1[pl.ds(side * half_ha, half_ha)] = spectrum.astype(jnp.bfloat16)

        if part == 0:
            pl.semaphore_wait(barrier, count - 1)

            @pl.loop(1, n_gz)
            def _(step):
                coef_copy((gz + step) % n_gz, gz).start()

        @pl.loop(0, half_ha * n_gz)
        def _(step):
            h = side * half_ha + (ha + 1 + step // n_gz) % half_ha
            g = (gz + 1 + step) % n_gz

            @pl.when(h * n_gz + g != me)
            def _():
                first_copy(h, g, ha, gz).start()

    own = pltpu.make_async_copy(send1.at[ha, gz], recv1.at[ha, gz], own_sem.at[0])
    own.start()
    own_coef = pltpu.make_async_copy(coef, coefs.at[gz], own_sem.at[1])
    own_coef.start()

    own_coef.wait()

    @pl.loop(1, n_gz)
    def _(step):
        g = (gz + step) % n_gz
        coef_copy(g, g).wait_recv()

    width = 4 * LANES
    channel = me * GROUP + lax.broadcasted_iota(jnp.int32, (GROUP, width), 0)
    spanwise = (channel % KYW).astype(jnp.float32)

    def spread(row):
        return jnp.tile(row, (GROUP, width // LANES))

    lower_of = lambda z: coefs[z // depth, pl.ds(z % depth, 1), :]
    upper_of = lambda z: coefs[z // depth, pl.ds(depth + z % depth, 1), :]

    @pl.loop(0, NX // width)
    def _(piece):
        at = pl.ds(pl.multiple_of(piece * width, width), width)
        column = piece * width + lax.broadcasted_iota(jnp.int32, (GROUP, width), 1)
        half = NX // 2
        wave_number = jnp.where(column <= half, column, column - half).astype(jnp.float32)
        damping = 1.0 + wavenumber_scale * (wave_number * wave_number + spanwise * spanwise)
        previous = None
        for z in range(z_total):
            lower, upper = spread(lower_of(z)), spread(upper_of(z))
            pivot = damping + (lower + upper)
            if z > 0:
                pivot = pivot + lower * previous
            inv = 1.0 / pivot
            inverse[pl.ds(z * GROUP, GROUP), at] = inv
            previous = -upper * inv
            upper_mod[pl.ds(z * GROUP, GROUP), at] = previous

    own.wait()
    x_load.wait()
    wave[...] = jnp.zeros_like(wave)

    @pl.loop(0, n_ha)
    def _(step):
        h = own_half_first(ha, step, n_ha)

        @pl.loop(0, n_gz)
        def _(g):
            @pl.when(h * n_gz + g != me)
            def _():
                first_copy(h, g, h, g).wait_recv()

        wave[...] += jnp.dot(
            recv1[h].reshape(bulk, rows),
            x_table[pl.ds(pl.multiple_of(h * rows, rows), rows), :],
            preferred_element_type=jnp.float32,
        )

    @pl.loop(0, NX // width)
    def _(piece):
        at = pl.ds(pl.multiple_of(piece * width, width), width)
        column = piece * width + lax.broadcasted_iota(jnp.int32, (GROUP, width), 1)
        weight = jnp.where(column % (NX // 2) == 0, 1.0, 2.0).astype(jnp.float32)
        value = None
        forward = []
        for z in range(z_total):
            source = wave[pl.ds(z * GROUP, GROUP), at]
            if z > 0:
                source = source + spread(lower_of(z)) * value
            value = source * inverse[pl.ds(z * GROUP, GROUP), at]
            wave[pl.ds(z * GROUP, GROUP), at] = value
        later = value * weight
        for z in range(z_total - 2, -1, -2):
            here = (
                wave[pl.ds(z * GROUP, GROUP), at] * weight
                - upper_mod[pl.ds(z * GROUP, GROUP), at] * later
            )
            solved[pl.ds(z * GROUP, 2 * GROUP), at] = jnp.concatenate(
                [here, later], 0
            ).astype(jnp.bfloat16)
            if z > 0:
                later = (
                    wave[pl.ds((z - 1) * GROUP, GROUP), at] * weight
                    - upper_mod[pl.ds((z - 1) * GROUP, GROUP), at] * here
                )

    @pl.loop(0, n_ha)
    def _(step):
        h = other_half_first(ha, step, n_ha)
        back = lax.dot_general(
            solved[...], x_table[pl.ds(pl.multiple_of(h * rows, rows), rows), :],
            (((1,), (1,)), ((), ())), preferred_element_type=jnp.float32,
        )
        send2[h] = back.astype(jnp.bfloat16).reshape(n_gz, block_rows, rows)

        @pl.loop(0, n_gz)
        def _(turn):
            g = (gz + 1 + turn) % n_gz

            @pl.when(h * n_gz + g != me)
            def _():
                second_copy(h, g, me).start()

    own_back = pltpu.make_async_copy(send2.at[ha, gz], recv2.at[me], own_sem.at[0])
    own_back.start()
    own_back.wait()

    @pl.loop(1, count)
    def _(step):
        peer = (me + step) % count
        second_copy(peer // n_gz, peer % n_gz, peer).wait_recv()

    for z in range(depth):
        part = recv2[:, pl.ds((z // 2) * 2 * GROUP, 2 * GROUP), :].astype(jnp.float32)
        part = part[:, (z % 2) * GROUP:(z % 2 + 1) * GROUP, :]
        out_ref[z] = part.reshape(count * GROUP, rows).astype(jnp.bfloat16)

    @pl.loop(1, count)
    def _(step):
        peer = (me + step) % count
        first_copy(peer // n_gz, peer % n_gz, ha, gz).wait_send()
        second_copy(peer // n_gz, peer % n_gz, me).wait_send()

    @pl.loop(1, n_gz)
    def _(step):
        coef_copy((gz + step) % n_gz, gz).wait_send()


def body_channels(n_ha, n_gz, velocity, lower_coef, upper_coef):
    depth, rows, _ = velocity.shape
    count = n_ha * n_gz
    bulk = depth * n_gz * GROUP
    block_rows = depth * GROUP
    cosine, sine = host_tables(NY, KYW)
    y_table = jnp.asarray(np.concatenate([cosine.T, -sine.T], 0), jnp.bfloat16)
    weight = np.where(np.arange(KYW) == 0, 1.0, 2.0)[:, None]
    back_table = jnp.asarray(
        np.concatenate([cosine.T * weight, -sine.T * weight], 0), jnp.bfloat16
    )
    x_table = real_x_table()
    hbm = pl.BlockSpec(memory_space=pl.ANY)
    smem = pl.BlockSpec(memory_space=pltpu.SMEM)
    dma = pltpu.SemaphoreType.DMA
    planes = pl.pallas_call(
        functools.partial(middle_kernel, n_ha, n_gz, depth),
        out_shape=jax.ShapeDtypeStruct((depth, count * GROUP, rows), jnp.bfloat16),
        in_specs=[hbm, hbm, hbm, smem, smem],
        out_specs=pl.BlockSpec(memory_space=pltpu.VMEM),
        scratch_shapes=[
            pltpu.VMEM(velocity.shape, jnp.bfloat16),
            pltpu.VMEM(y_table.shape, jnp.bfloat16),
            pltpu.VMEM(x_table.shape, jnp.bfloat16),
            pltpu.VMEM((n_ha, n_gz, block_rows, rows), jnp.bfloat16),
            pltpu.VMEM((n_ha, n_gz, block_rows, rows), jnp.bfloat16),
            pltpu.VMEM((bulk, NX), jnp.float32),
            pltpu.VMEM((bulk, NX), jnp.float32),
            pltpu.VMEM((bulk, NX), jnp.float32),
            pltpu.VMEM((bulk, NX), jnp.bfloat16),
            pltpu.VMEM((n_ha, n_gz, block_rows, rows), jnp.bfloat16),
            pltpu.VMEM((count, block_rows, rows), jnp.bfloat16),
            pltpu.VMEM((2 * depth, LANES), jnp.float32),
            pltpu.VMEM((n_gz, 2 * depth, LANES), jnp.float32),
            dma((depth + 1,)), dma, dma((2,)),
            dma((count,)), dma((count,)), dma((count,)), dma((count,)),
            dma((n_gz,)), dma((n_gz,)),
        ],
        compiler_params=pltpu.CompilerParams(
            collective_id=0, has_side_effects=True, vmem_limit_bytes=48 * 1024 * 1024
        ),
    )(velocity, y_table, x_table, lower_coef, upper_coef)
    result = jnp.einsum("zkx,ky->zxy", planes, back_table, preferred_element_type=jnp.float32)
    return result.astype(jnp.bfloat16)


def solution(mesh):
    n_ha, n_gz = mesh.shape["ha"], mesh.shape["gz"]
    by_channel = (
        2 * KYW == n_ha * n_gz * GROUP
        and n_ha % 2 == 0
        and NX % (n_ha * LANES) == 0
    )
    body = functools.partial(body_channels, n_ha, n_gz) if by_channel else body_general
    in_specs = (P("gz", "ha", None), P("gz"), P("gz"))
    out_specs = P("gz", "ha", None)
    return jax.shard_map(body, mesh=mesh, in_specs=in_specs, out_specs=out_specs, check_vma=False)
```

```python
import functools
import math

import jax
import jax.numpy as jnp
import numpy as np
from jax import lax
from jax.experimental import pallas as pl
from jax.experimental.pallas import tpu as pltpu
from jax.sharding import PartitionSpec as P

NX = 2048
NY = 2048
KYW = 128
GROUP = 8
LANES = 128


wavenumber_scale = 0.001


def tables(length, mode_count):
    position = jnp.arange(length, dtype=jnp.int32)[:, None]
    wave_index = jnp.arange(mode_count, dtype=jnp.int32)[None, :]
    angles = (position * wave_index % length).astype(jnp.float32) * (2.0 * math.pi / length)
    factor = 1.0 / math.sqrt(length)
    return (
        (jnp.cos(angles) * factor).astype(jnp.bfloat16),
        (jnp.sin(angles) * factor).astype(jnp.bfloat16),
    )


def signed_wave(lane_index):
    return jnp.where(lane_index < NX // 2, lane_index, lane_index - NX).astype(jnp.float32)


def damping_for(kx_value, spanwise_wave_value):
    return 1.0 + wavenumber_scale * (
        kx_value[None, :] * kx_value[None, :]
        + spanwise_wave_value[:, None] * spanwise_wave_value[:, None]
    )


def band_pair(lower_coef, upper_coef, z_global, z_total):
    sub_coef = jnp.where(z_global == 0, jnp.zeros_like(lower_coef), -lower_coef)
    sup_coef = jnp.where(z_global == z_total - 1, jnp.zeros_like(upper_coef), -upper_coef)
    return (sub_coef, sup_coef)


def thomas(lower_band, main_band, upper_band, source):

    def forward(running, packed):
        upper_prev, previous_source = running
        lower_row, main_row, upper_row, source_row = packed
        inverse = 1.0 / (main_row - lower_row * upper_prev)
        upper_new = upper_row * inverse
        source_new = (source_row - lower_row[None] * previous_source) * inverse[None]
        return ((upper_new, source_new), (upper_new, source_new))

    initial = (jnp.zeros_like(main_band[0]), jnp.zeros_like(source[0]))
    unused, (upper_mod, source_mod) = lax.scan(
        forward, initial, (lower_band, main_band, upper_band, source)
    )

    def backward(running, packed):
        upper_row, source_row = packed
        result = source_row - upper_row[None] * running
        return (result, result)

    unused, solved = lax.scan(
        backward, jnp.zeros_like(source[0]), (upper_mod, source_mod), reverse=True
    )
    return solved


def body_general(velocity, lower_coef, upper_coef):
    depth_rows = velocity.shape[0]
    z_groups = lax.axis_size("gz")
    z_total = depth_rows * z_groups
    wave_count = KYW // lax.axis_size("ha")
    y_cosine, y_sine = tables(NY, KYW)
    x_cosine, x_sine = tables(NX, NX)
    spec_re = jnp.einsum("zxy,yk->zkx", velocity, y_cosine, preferred_element_type=jnp.float32)
    spec_im = -jnp.einsum("zxy,yk->zkx", velocity, y_sine, preferred_element_type=jnp.float32)
    spectrum = jnp.stack([spec_re, spec_im], 1).astype(jnp.bfloat16)
    block = lax.all_to_all(spectrum, "ha", split_axis=2, concat_axis=3, tiled=True)
    with_cos = jnp.dot(block, x_cosine, preferred_element_type=jnp.float32)
    with_sin = jnp.dot(block, x_sine, preferred_element_type=jnp.float32)
    source = jnp.stack([with_cos[:, 0] + with_sin[:, 1], with_cos[:, 1] - with_sin[:, 0]], 1)
    spanwise_wave_value = (
        lax.axis_index("ha") * wave_count + jnp.arange(wave_count, dtype=jnp.int32)
    ).astype(jnp.float32)
    lower_all, upper_all = (
        lax.all_gather(lower_coef, "gz", axis=0, tiled=True),
        lax.all_gather(upper_coef, "gz", axis=0, tiled=True),
    )
    columns = lax.all_to_all(source, "gz", split_axis=3, concat_axis=0, tiled=True)
    lane_count = NX // z_groups
    lane_index = lax.axis_index("gz") * lane_count + jnp.arange(lane_count, dtype=jnp.int32)
    z_every = jnp.arange(z_total, dtype=jnp.int32)
    sub_coef, sup_coef = band_pair(lower_all, upper_all, z_every, z_total)
    main_band = (
        damping_for(signed_wave(lane_index), spanwise_wave_value)[None]
        + (lower_all + upper_all)[:, None, None]
    )
    sub_band = jnp.broadcast_to(sub_coef[:, None, None], main_band.shape)
    sup_band = jnp.broadcast_to(sup_coef[:, None, None], main_band.shape)
    solved_columns = thomas(sub_band, main_band, sup_band, columns)
    solved = lax.all_to_all(
        solved_columns.astype(jnp.bfloat16), "gz", split_axis=0, concat_axis=3, tiled=True
    ).astype(solved_columns.dtype)
    rounded = solved.astype(jnp.bfloat16)
    part_cos = jnp.dot(rounded, x_cosine, preferred_element_type=jnp.float32)
    part_sin = jnp.dot(rounded, x_sine, preferred_element_type=jnp.float32)
    planes = jnp.stack(
        [part_cos[:, 0] - part_sin[:, 1], part_cos[:, 1] + part_sin[:, 0]], 1
    ).astype(jnp.bfloat16)
    weight = jnp.where(jnp.arange(KYW, dtype=jnp.int32) == 0, 1.0, 2.0).astype(jnp.float32)
    w_cosine = (y_cosine.astype(jnp.float32) * weight[None, :]).astype(jnp.bfloat16)
    w_sine = (y_sine.astype(jnp.float32) * weight[None, :]).astype(jnp.bfloat16)
    block = lax.all_to_all(planes, "ha", split_axis=3, concat_axis=2, tiled=True)
    result = jnp.einsum("nkx,yk->nxy", block[:, 0], w_cosine, preferred_element_type=jnp.float32)
    result = result - jnp.einsum(
        "nkx,yk->nxy", block[:, 1], w_sine, preferred_element_type=jnp.float32
    )
    return result.astype(jnp.bfloat16)


def host_tables(length, mode_count):
    position = np.arange(length)[:, None]
    wave_index = np.arange(mode_count)[None, :]
    angles = (position * wave_index % length) * (2.0 * math.pi / length)
    factor = 1.0 / math.sqrt(length)
    return np.cos(angles) * factor, np.sin(angles) * factor


def real_x_table():
    cosine, sine = host_tables(NX, NX // 2 + 1)
    half = NX // 2
    table = np.concatenate([cosine[:, :half], sine[:, :half]], 1)
    table[:, half] = cosine[:, half]
    return jnp.asarray(table, jnp.bfloat16)


def other_half_first(position, step, count):
    half = count // 2
    side = position // half
    base = jnp.where(step < half, (1 - side) * half, side * half)
    return base + (position + 1 + step) % half


def own_half_first(position, step, count):
    half = count // 2
    side = position // half
    base = jnp.where(step < half, side * half, (1 - side) * half)
    return base + (position + step) % half


def middle_kernel(
    n_ha, n_gz, depth,
    velocity_ref, y_table_ref, x_table_ref, lower_ref, upper_ref,
    out_ref,
    velocity, y_table, x_table, send1, recv1, wave, inverse, upper_mod, solved,
    send2, recv2, coef, coefs,
    load_sem, table_sem, own_sem,
    send1_sem, recv1_sem, send2_sem, recv2_sem, coef_send_sem, coef_recv_sem,
):
    ha = lax.axis_index("ha")
    gz = lax.axis_index("gz")
    count = n_ha * n_gz
    me = ha * n_gz + gz
    rows = velocity.shape[1]
    z_total = depth * n_gz
    block_rows = depth * GROUP
    bulk = z_total * GROUP

    y_load = pltpu.make_async_copy(y_table_ref, y_table, load_sem.at[depth])
    y_load.start()
    loads = []
    for z in range(depth):
        load = pltpu.make_async_copy(velocity_ref.at[z], velocity.at[z], load_sem.at[z])
        load.start()
        loads.append(load)
    x_load = pltpu.make_async_copy(x_table_ref, x_table, table_sem)
    x_load.start()

    barrier = pltpu.get_barrier_semaphore()

    @pl.loop(1, count)
    def _(step):
        peer = (me + step) % count
        pl.semaphore_signal(
            barrier, inc=1, device_id={"ha": peer // n_gz, "gz": peer % n_gz},
            device_id_type=pl.DeviceIdType.MESH,
        )

    for z in range(depth):
        coef[pl.ds(z, 1), :] = jnp.full((1, LANES), lower_ref[z], jnp.float32)
        coef[pl.ds(depth + z, 1), :] = jnp.full((1, LANES), upper_ref[z], jnp.float32)

    def first_copy(h, g, slot_h, slot_g):
        return pltpu.make_async_remote_copy(
            src_ref=send1.at[h, g],
            dst_ref=recv1.at[slot_h, slot_g],
            send_sem=send1_sem.at[h * n_gz + g],
            recv_sem=recv1_sem.at[slot_h * n_gz + slot_g],
            device_id={"ha": h, "gz": g},
            device_id_type=pl.DeviceIdType.MESH,
        )

    def second_copy(h, g, slot):
        return pltpu.make_async_remote_copy(
            src_ref=send2.at[h, g],
            dst_ref=recv2.at[slot],
            send_sem=send2_sem.at[h * n_gz + g],
            recv_sem=recv2_sem.at[slot],
            device_id={"ha": h, "gz": g},
            device_id_type=pl.DeviceIdType.MESH,
        )

    def coef_copy(g, slot):
        return pltpu.make_async_remote_copy(
            src_ref=coef,
            dst_ref=coefs.at[slot],
            send_sem=coef_send_sem.at[g],
            recv_sem=coef_recv_sem.at[slot],
            device_id={"ha": ha, "gz": g},
            device_id_type=pl.DeviceIdType.MESH,
        )

    y_load.wait()
    for pair in range(0, depth, 2):
        planes = []
        for z in range(pair, pair + 2):
            loads[z].wait()
            planes.append(
                lax.dot_general(
                    y_table[...], velocity[z],
                    (((1,), (1,)), ((), ())), preferred_element_type=jnp.float32,
                ).reshape(n_ha, n_gz, 1, GROUP, rows)
            )
        spectrum = jnp.concatenate(planes, 2).reshape(n_ha, n_gz, 2 * GROUP, rows)
        send1[:, :, pl.ds(pair * GROUP, 2 * GROUP), :] = spectrum.astype(jnp.bfloat16)

    pl.semaphore_wait(barrier, count - 1)

    @pl.loop(1, n_gz)
    def _(step):
        coef_copy((gz + step) % n_gz, gz).start()

    @pl.loop(0, count)
    def _(step):
        h = other_half_first(ha, step // n_gz, n_ha)
        g = (gz + 1 + step) % n_gz

        @pl.when(h * n_gz + g != me)
        def _():
            first_copy(h, g, ha, gz).start()

    own = pltpu.make_async_copy(send1.at[ha, gz], recv1.at[ha, gz], own_sem.at[0])
    own.start()
    own_coef = pltpu.make_async_copy(coef, coefs.at[gz], own_sem.at[1])
    own_coef.start()

    own_coef.wait()

    @pl.loop(1, n_gz)
    def _(step):
        g = (gz + step) % n_gz
        coef_copy(g, g).wait_recv()

    width = 4 * LANES
    channel = me * GROUP + lax.broadcasted_iota(jnp.int32, (GROUP, width), 0)
    spanwise = (channel % KYW).astype(jnp.float32)

    def spread(row):
        return jnp.tile(row, (GROUP, width // LANES))

    lower_of = lambda z: coefs[z // depth, pl.ds(z % depth, 1), :]
    upper_of = lambda z: coefs[z // depth, pl.ds(depth + z % depth, 1), :]

    @pl.loop(0, NX // width)
    def _(piece):
        at = pl.ds(pl.multiple_of(piece * width, width), width)
        column = piece * width + lax.broadcasted_iota(jnp.int32, (GROUP, width), 1)
        half = NX // 2
        wave_number = jnp.where(column <= half, column, column - half).astype(jnp.float32)
        damping = 1.0 + wavenumber_scale * (wave_number * wave_number + spanwise * spanwise)
        previous = None
        for z in range(z_total):
            lower, upper = spread(lower_of(z)), spread(upper_of(z))
            pivot = damping + (lower + upper)
            if z > 0:
                pivot = pivot + lower * previous
            inv = 1.0 / pivot
            inverse[pl.ds(z * GROUP, GROUP), at] = inv
            previous = -upper * inv
            upper_mod[pl.ds(z * GROUP, GROUP), at] = previous

    own.wait()
    x_load.wait()
    wave[...] = jnp.zeros_like(wave)

    @pl.loop(0, n_ha)
    def _(step):
        h = own_half_first(ha, step, n_ha)

        @pl.loop(0, n_gz)
        def _(g):
            @pl.when(h * n_gz + g != me)
            def _():
                first_copy(h, g, h, g).wait_recv()

        wave[...] += jnp.dot(
            recv1[h].reshape(bulk, rows),
            x_table[pl.ds(pl.multiple_of(h * rows, rows), rows), :],
            preferred_element_type=jnp.float32,
        )

    @pl.loop(0, NX // width)
    def _(piece):
        at = pl.ds(pl.multiple_of(piece * width, width), width)
        column = piece * width + lax.broadcasted_iota(jnp.int32, (GROUP, width), 1)
        weight = jnp.where(column % (NX // 2) == 0, 1.0, 2.0).astype(jnp.float32)
        value = None
        forward = []
        for z in range(z_total):
            source = wave[pl.ds(z * GROUP, GROUP), at]
            if z > 0:
                source = source + spread(lower_of(z)) * value
            value = source * inverse[pl.ds(z * GROUP, GROUP), at]
            wave[pl.ds(z * GROUP, GROUP), at] = value
        later = value * weight
        for z in range(z_total - 2, -1, -2):
            here = (
                wave[pl.ds(z * GROUP, GROUP), at] * weight
                - upper_mod[pl.ds(z * GROUP, GROUP), at] * later
            )
            solved[pl.ds(z * GROUP, 2 * GROUP), at] = jnp.concatenate(
                [here, later], 0
            ).astype(jnp.bfloat16)
            if z > 0:
                later = (
                    wave[pl.ds((z - 1) * GROUP, GROUP), at] * weight
                    - upper_mod[pl.ds((z - 1) * GROUP, GROUP), at] * here
                )

    @pl.loop(0, n_ha)
    def _(step):
        h = other_half_first(ha, step, n_ha)
        back = lax.dot_general(
            solved[...], x_table[pl.ds(pl.multiple_of(h * rows, rows), rows), :],
            (((1,), (1,)), ((), ())), preferred_element_type=jnp.float32,
        )
        send2[h] = back.astype(jnp.bfloat16).reshape(n_gz, block_rows, rows)

        @pl.loop(0, n_gz)
        def _(turn):
            g = (gz + 1 + turn) % n_gz

            @pl.when(h * n_gz + g != me)
            def _():
                second_copy(h, g, me).start()

    own_back = pltpu.make_async_copy(send2.at[ha, gz], recv2.at[me], own_sem.at[0])
    own_back.start()
    own_back.wait()

    @pl.loop(1, count)
    def _(step):
        peer = (me + step) % count
        second_copy(peer // n_gz, peer % n_gz, peer).wait_recv()

    for z in range(depth):
        part = recv2[:, pl.ds((z // 2) * 2 * GROUP, 2 * GROUP), :].astype(jnp.float32)
        part = part[:, (z % 2) * GROUP:(z % 2 + 1) * GROUP, :]
        out_ref[z] = part.reshape(count * GROUP, rows).astype(jnp.bfloat16)

    @pl.loop(1, count)
    def _(step):
        peer = (me + step) % count
        first_copy(peer // n_gz, peer % n_gz, ha, gz).wait_send()
        second_copy(peer // n_gz, peer % n_gz, me).wait_send()

    @pl.loop(1, n_gz)
    def _(step):
        coef_copy((gz + step) % n_gz, gz).wait_send()


def body_channels(n_ha, n_gz, velocity, lower_coef, upper_coef):
    depth, rows, _ = velocity.shape
    count = n_ha * n_gz
    bulk = depth * n_gz * GROUP
    block_rows = depth * GROUP
    cosine, sine = host_tables(NY, KYW)
    y_table = jnp.asarray(np.concatenate([cosine.T, -sine.T], 0), jnp.bfloat16)
    weight = np.where(np.arange(KYW) == 0, 1.0, 2.0)[:, None]
    back_table = jnp.asarray(
        np.concatenate([cosine.T * weight, -sine.T * weight], 0), jnp.bfloat16
    )
    x_table = real_x_table()
    hbm = pl.BlockSpec(memory_space=pl.ANY)
    smem = pl.BlockSpec(memory_space=pltpu.SMEM)
    dma = pltpu.SemaphoreType.DMA
    planes = pl.pallas_call(
        functools.partial(middle_kernel, n_ha, n_gz, depth),
        out_shape=jax.ShapeDtypeStruct((depth, count * GROUP, rows), jnp.bfloat16),
        in_specs=[hbm, hbm, hbm, smem, smem],
        out_specs=pl.BlockSpec(memory_space=pltpu.VMEM),
        scratch_shapes=[
            pltpu.VMEM(velocity.shape, jnp.bfloat16),
            pltpu.VMEM(y_table.shape, jnp.bfloat16),
            pltpu.VMEM(x_table.shape, jnp.bfloat16),
            pltpu.VMEM((n_ha, n_gz, block_rows, rows), jnp.bfloat16),
            pltpu.VMEM((n_ha, n_gz, block_rows, rows), jnp.bfloat16),
            pltpu.VMEM((bulk, NX), jnp.float32),
            pltpu.VMEM((bulk, NX), jnp.float32),
            pltpu.VMEM((bulk, NX), jnp.float32),
            pltpu.VMEM((bulk, NX), jnp.bfloat16),
            pltpu.VMEM((n_ha, n_gz, block_rows, rows), jnp.bfloat16),
            pltpu.VMEM((count, block_rows, rows), jnp.bfloat16),
            pltpu.VMEM((2 * depth, LANES), jnp.float32),
            pltpu.VMEM((n_gz, 2 * depth, LANES), jnp.float32),
            dma((depth + 1,)), dma, dma((2,)),
            dma((count,)), dma((count,)), dma((count,)), dma((count,)),
            dma((n_gz,)), dma((n_gz,)),
        ],
        compiler_params=pltpu.CompilerParams(
            collective_id=0, has_side_effects=True, vmem_limit_bytes=60 * 1024 * 1024
        ),
    )(velocity, y_table, x_table, lower_coef, upper_coef)
    result = jnp.einsum("zkx,ky->zxy", planes, back_table, preferred_element_type=jnp.float32)
    return result.astype(jnp.bfloat16)


def solution(mesh):
    n_ha, n_gz = mesh.shape["ha"], mesh.shape["gz"]
    by_channel = (
        2 * KYW == n_ha * n_gz * GROUP
        and n_ha % 2 == 0
        and NX % (n_ha * LANES) == 0
    )
    body = functools.partial(body_channels, n_ha, n_gz) if by_channel else body_general
    in_specs = (P("gz", "ha", None), P("gz"), P("gz"))
    out_specs = P("gz", "ha", None)
    return jax.shard_map(body, mesh=mesh, in_specs=in_specs, out_specs=out_specs, check_vma=False)
```

```python
import functools
import math

import jax
import jax.numpy as jnp
import numpy as np
from jax import lax
from jax.experimental import pallas as pl
from jax.experimental.pallas import tpu as pltpu
from jax.sharding import PartitionSpec as P

NX = 2048
NY = 2048
KYW = 128
GROUP = 8
LANES = 128


wavenumber_scale = 0.001


def tables(length, mode_count):
    position = jnp.arange(length, dtype=jnp.int32)[:, None]
    wave_index = jnp.arange(mode_count, dtype=jnp.int32)[None, :]
    angles = (position * wave_index % length).astype(jnp.float32) * (2.0 * math.pi / length)
    factor = 1.0 / math.sqrt(length)
    return (
        (jnp.cos(angles) * factor).astype(jnp.bfloat16),
        (jnp.sin(angles) * factor).astype(jnp.bfloat16),
    )


def signed_wave(lane_index):
    return jnp.where(lane_index < NX // 2, lane_index, lane_index - NX).astype(jnp.float32)


def damping_for(kx_value, spanwise_wave_value):
    return 1.0 + wavenumber_scale * (
        kx_value[None, :] * kx_value[None, :]
        + spanwise_wave_value[:, None] * spanwise_wave_value[:, None]
    )


def band_pair(lower_coef, upper_coef, z_global, z_total):
    sub_coef = jnp.where(z_global == 0, jnp.zeros_like(lower_coef), -lower_coef)
    sup_coef = jnp.where(z_global == z_total - 1, jnp.zeros_like(upper_coef), -upper_coef)
    return (sub_coef, sup_coef)


def thomas(lower_band, main_band, upper_band, source):

    def forward(running, packed):
        upper_prev, previous_source = running
        lower_row, main_row, upper_row, source_row = packed
        inverse = 1.0 / (main_row - lower_row * upper_prev)
        upper_new = upper_row * inverse
        source_new = (source_row - lower_row[None] * previous_source) * inverse[None]
        return ((upper_new, source_new), (upper_new, source_new))

    initial = (jnp.zeros_like(main_band[0]), jnp.zeros_like(source[0]))
    unused, (upper_mod, source_mod) = lax.scan(
        forward, initial, (lower_band, main_band, upper_band, source)
    )

    def backward(running, packed):
        upper_row, source_row = packed
        result = source_row - upper_row[None] * running
        return (result, result)

    unused, solved = lax.scan(
        backward, jnp.zeros_like(source[0]), (upper_mod, source_mod), reverse=True
    )
    return solved


def body_general(velocity, lower_coef, upper_coef):
    depth_rows = velocity.shape[0]
    z_groups = lax.axis_size("gz")
    z_total = depth_rows * z_groups
    wave_count = KYW // lax.axis_size("ha")
    y_cosine, y_sine = tables(NY, KYW)
    x_cosine, x_sine = tables(NX, NX)
    spec_re = jnp.einsum("zxy,yk->zkx", velocity, y_cosine, preferred_element_type=jnp.float32)
    spec_im = -jnp.einsum("zxy,yk->zkx", velocity, y_sine, preferred_element_type=jnp.float32)
    spectrum = jnp.stack([spec_re, spec_im], 1).astype(jnp.bfloat16)
    block = lax.all_to_all(spectrum, "ha", split_axis=2, concat_axis=3, tiled=True)
    with_cos = jnp.dot(block, x_cosine, preferred_element_type=jnp.float32)
    with_sin = jnp.dot(block, x_sine, preferred_element_type=jnp.float32)
    source = jnp.stack([with_cos[:, 0] + with_sin[:, 1], with_cos[:, 1] - with_sin[:, 0]], 1)
    spanwise_wave_value = (
        lax.axis_index("ha") * wave_count + jnp.arange(wave_count, dtype=jnp.int32)
    ).astype(jnp.float32)
    lower_all, upper_all = (
        lax.all_gather(lower_coef, "gz", axis=0, tiled=True),
        lax.all_gather(upper_coef, "gz", axis=0, tiled=True),
    )
    columns = lax.all_to_all(source, "gz", split_axis=3, concat_axis=0, tiled=True)
    lane_count = NX // z_groups
    lane_index = lax.axis_index("gz") * lane_count + jnp.arange(lane_count, dtype=jnp.int32)
    z_every = jnp.arange(z_total, dtype=jnp.int32)
    sub_coef, sup_coef = band_pair(lower_all, upper_all, z_every, z_total)
    main_band = (
        damping_for(signed_wave(lane_index), spanwise_wave_value)[None]
        + (lower_all + upper_all)[:, None, None]
    )
    sub_band = jnp.broadcast_to(sub_coef[:, None, None], main_band.shape)
    sup_band = jnp.broadcast_to(sup_coef[:, None, None], main_band.shape)
    solved_columns = thomas(sub_band, main_band, sup_band, columns)
    solved = lax.all_to_all(
        solved_columns.astype(jnp.bfloat16), "gz", split_axis=0, concat_axis=3, tiled=True
    ).astype(solved_columns.dtype)
    rounded = solved.astype(jnp.bfloat16)
    part_cos = jnp.dot(rounded, x_cosine, preferred_element_type=jnp.float32)
    part_sin = jnp.dot(rounded, x_sine, preferred_element_type=jnp.float32)
    planes = jnp.stack(
        [part_cos[:, 0] - part_sin[:, 1], part_cos[:, 1] + part_sin[:, 0]], 1
    ).astype(jnp.bfloat16)
    weight = jnp.where(jnp.arange(KYW, dtype=jnp.int32) == 0, 1.0, 2.0).astype(jnp.float32)
    w_cosine = (y_cosine.astype(jnp.float32) * weight[None, :]).astype(jnp.bfloat16)
    w_sine = (y_sine.astype(jnp.float32) * weight[None, :]).astype(jnp.bfloat16)
    block = lax.all_to_all(planes, "ha", split_axis=3, concat_axis=2, tiled=True)
    result = jnp.einsum("nkx,yk->nxy", block[:, 0], w_cosine, preferred_element_type=jnp.float32)
    result = result - jnp.einsum(
        "nkx,yk->nxy", block[:, 1], w_sine, preferred_element_type=jnp.float32
    )
    return result.astype(jnp.bfloat16)


def host_tables(length, mode_count):
    position = np.arange(length)[:, None]
    wave_index = np.arange(mode_count)[None, :]
    angles = (position * wave_index % length) * (2.0 * math.pi / length)
    factor = 1.0 / math.sqrt(length)
    return np.cos(angles) * factor, np.sin(angles) * factor


def real_x_table():
    cosine, sine = host_tables(NX, NX // 2 + 1)
    half = NX // 2
    table = np.concatenate([cosine[:, :half], sine[:, :half]], 1)
    table[:, half] = cosine[:, half]
    return jnp.asarray(table, jnp.bfloat16)


def other_half_first(position, step, count):
    half = count // 2
    side = position // half
    base = jnp.where(step < half, (1 - side) * half, side * half)
    return base + (position + 1 + step) % half


def own_half_first(position, step, count):
    half = count // 2
    side = position // half
    base = jnp.where(step < half, side * half, (1 - side) * half)
    return base + (position + step) % half


def middle_kernel(
    n_ha, n_gz, depth,
    velocity_ref, y_table_ref, x_table_ref, lower_ref, upper_ref,
    out_ref,
    velocity, y_table, x_table, send1, recv1, wave, inverse, upper_mod, solved,
    send2, recv2, coef, coefs,
    load_sem, table_sem, own_sem,
    send1_sem, recv1_sem, send2_sem, recv2_sem, coef_send_sem, coef_recv_sem,
):
    ha = lax.axis_index("ha")
    gz = lax.axis_index("gz")
    count = n_ha * n_gz
    me = ha * n_gz + gz
    rows = velocity.shape[1]
    z_total = depth * n_gz
    block_rows = depth * GROUP
    bulk = z_total * GROUP

    y_load = pltpu.make_async_copy(y_table_ref, y_table, load_sem.at[depth])
    y_load.start()
    loads = []
    for z in range(depth):
        load = pltpu.make_async_copy(velocity_ref.at[z], velocity.at[z], load_sem.at[z])
        load.start()
        loads.append(load)
    x_load = pltpu.make_async_copy(x_table_ref, x_table, table_sem)
    x_load.start()

    barrier = pltpu.get_barrier_semaphore()

    @pl.loop(1, count)
    def _(step):
        peer = (me + step) % count
        pl.semaphore_signal(
            barrier, inc=1, device_id={"ha": peer // n_gz, "gz": peer % n_gz},
            device_id_type=pl.DeviceIdType.MESH,
        )

    for z in range(depth):
        coef[pl.ds(z, 1), :] = jnp.full((1, LANES), lower_ref[z], jnp.float32)
        coef[pl.ds(depth + z, 1), :] = jnp.full((1, LANES), upper_ref[z], jnp.float32)

    def first_copy(h, g, slot_h, slot_g):
        return pltpu.make_async_remote_copy(
            src_ref=send1.at[h, g],
            dst_ref=recv1.at[slot_h, slot_g],
            send_sem=send1_sem.at[h * n_gz + g],
            recv_sem=recv1_sem.at[slot_h * n_gz + slot_g],
            device_id={"ha": h, "gz": g},
            device_id_type=pl.DeviceIdType.MESH,
        )

    def second_copy(h, g, slot):
        return pltpu.make_async_remote_copy(
            src_ref=send2.at[h, g],
            dst_ref=recv2.at[slot],
            send_sem=send2_sem.at[h * n_gz + g],
            recv_sem=recv2_sem.at[slot],
            device_id={"ha": h, "gz": g},
            device_id_type=pl.DeviceIdType.MESH,
        )

    def coef_copy(g, slot):
        return pltpu.make_async_remote_copy(
            src_ref=coef,
            dst_ref=coefs.at[slot],
            send_sem=coef_send_sem.at[g],
            recv_sem=coef_recv_sem.at[slot],
            device_id={"ha": ha, "gz": g},
            device_id_type=pl.DeviceIdType.MESH,
        )

    y_load.wait()
    for pair in range(0, depth, 2):
        planes = []
        for z in range(pair, pair + 2):
            loads[z].wait()
            planes.append(
                lax.dot_general(
                    y_table[...], velocity[z],
                    (((1,), (1,)), ((), ())), preferred_element_type=jnp.float32,
                ).reshape(n_ha, n_gz, 1, GROUP, rows)
            )
        spectrum = jnp.concatenate(planes, 2).reshape(n_ha, n_gz, 2 * GROUP, rows)
        send1[:, :, pl.ds(pair * GROUP, 2 * GROUP), :] = spectrum.astype(jnp.bfloat16)

    pl.semaphore_wait(barrier, count - 1)

    @pl.loop(1, n_gz)
    def _(step):
        coef_copy((gz + step) % n_gz, gz).start()

    @pl.loop(1, count)
    def _(step):
        peer = (me + step) % count
        first_copy(peer // n_gz, peer % n_gz, ha, gz).start()

    own = pltpu.make_async_copy(send1.at[ha, gz], recv1.at[ha, gz], own_sem.at[0])
    own.start()
    own_coef = pltpu.make_async_copy(coef, coefs.at[gz], own_sem.at[1])
    own_coef.start()

    own_coef.wait()

    @pl.loop(1, n_gz)
    def _(step):
        g = (gz + step) % n_gz
        coef_copy(g, g).wait_recv()

    width = 4 * LANES
    channel = me * GROUP + lax.broadcasted_iota(jnp.int32, (GROUP, width), 0)
    spanwise = (channel % KYW).astype(jnp.float32)

    def spread(row):
        return jnp.tile(row, (GROUP, width // LANES))

    lower_of = lambda z: coefs[z // depth, pl.ds(z % depth, 1), :]
    upper_of = lambda z: coefs[z // depth, pl.ds(depth + z % depth, 1), :]

    @pl.loop(0, NX // width)
    def _(piece):
        at = pl.ds(pl.multiple_of(piece * width, width), width)
        column = piece * width + lax.broadcasted_iota(jnp.int32, (GROUP, width), 1)
        half = NX // 2
        wave_number = jnp.where(column <= half, column, column - half).astype(jnp.float32)
        damping = 1.0 + wavenumber_scale * (wave_number * wave_number + spanwise * spanwise)
        previous = None
        for z in range(z_total):
            lower, upper = spread(lower_of(z)), spread(upper_of(z))
            pivot = damping + (lower + upper)
            if z > 0:
                pivot = pivot + lower * previous
            inv = 1.0 / pivot
            inverse[pl.ds(z * GROUP, GROUP), at] = inv
            previous = -upper * inv
            upper_mod[pl.ds(z * GROUP, GROUP), at] = previous

    own.wait()
    x_load.wait()
    wave[...] = jnp.zeros_like(wave)

    @pl.loop(0, n_ha)
    def _(step):
        h = own_half_first(ha, step, n_ha)

        @pl.loop(0, n_gz)
        def _(g):
            @pl.when(h * n_gz + g != me)
            def _():
                first_copy(h, g, h, g).wait_recv()

        wave[...] += jnp.dot(
            recv1[h].reshape(bulk, rows),
            x_table[pl.ds(pl.multiple_of(h * rows, rows), rows), :],
            preferred_element_type=jnp.float32,
        )

    @pl.loop(0, NX // width)
    def _(piece):
        at = pl.ds(pl.multiple_of(piece * width, width), width)
        column = piece * width + lax.broadcasted_iota(jnp.int32, (GROUP, width), 1)
        weight = jnp.where(column % (NX // 2) == 0, 1.0, 2.0).astype(jnp.float32)
        value = None
        forward = []
        for z in range(z_total):
            source = wave[pl.ds(z * GROUP, GROUP), at]
            if z > 0:
                source = source + spread(lower_of(z)) * value
            value = source * inverse[pl.ds(z * GROUP, GROUP), at]
            wave[pl.ds(z * GROUP, GROUP), at] = value
        later = value * weight
        for z in range(z_total - 2, -1, -2):
            here = (
                wave[pl.ds(z * GROUP, GROUP), at] * weight
                - upper_mod[pl.ds(z * GROUP, GROUP), at] * later
            )
            solved[pl.ds(z * GROUP, 2 * GROUP), at] = jnp.concatenate(
                [here, later], 0
            ).astype(jnp.bfloat16)
            if z > 0:
                later = (
                    wave[pl.ds((z - 1) * GROUP, GROUP), at] * weight
                    - upper_mod[pl.ds((z - 1) * GROUP, GROUP), at] * here
                )

    @pl.loop(0, n_ha)
    def _(step):
        h = other_half_first(ha, step, n_ha)
        back = lax.dot_general(
            solved[...], x_table[pl.ds(pl.multiple_of(h * rows, rows), rows), :],
            (((1,), (1,)), ((), ())), preferred_element_type=jnp.float32,
        )
        send2[h] = back.astype(jnp.bfloat16).reshape(n_gz, block_rows, rows)

        @pl.loop(0, n_gz)
        def _(turn):
            g = (gz + 1 + turn) % n_gz

            @pl.when(h * n_gz + g != me)
            def _():
                second_copy(h, g, me).start()

    own_back = pltpu.make_async_copy(send2.at[ha, gz], recv2.at[me], own_sem.at[0])
    own_back.start()
    own_back.wait()

    @pl.loop(0, count // 2)
    def _(step):
        pair = (me // 2 + 1 + step) % (count // 2)
        for member in range(2):
            source = pair * 2 + member

            @pl.when(source != me)
            def _():
                second_copy(source // n_gz, source % n_gz, source).wait_recv()

        even = recv2[pair * 2].astype(jnp.float32)
        odd = recv2[pair * 2 + 1].astype(jnp.float32)
        at = pl.ds(pl.multiple_of(pair * 2 * GROUP, 2 * GROUP), 2 * GROUP)
        for z in range(depth):
            own_z = slice(z * GROUP, (z + 1) * GROUP)
            out_ref[z, at, :] = jnp.concatenate([even[own_z], odd[own_z]], 0).astype(jnp.bfloat16)

    @pl.loop(1, count)
    def _(step):
        peer = (me + step) % count
        first_copy(peer // n_gz, peer % n_gz, ha, gz).wait_send()
        second_copy(peer // n_gz, peer % n_gz, me).wait_send()

    @pl.loop(1, n_gz)
    def _(step):
        coef_copy((gz + step) % n_gz, gz).wait_send()


def body_channels(n_ha, n_gz, velocity, lower_coef, upper_coef):
    depth, rows, _ = velocity.shape
    count = n_ha * n_gz
    bulk = depth * n_gz * GROUP
    block_rows = depth * GROUP
    cosine, sine = host_tables(NY, KYW)
    y_table = jnp.asarray(np.concatenate([cosine.T, -sine.T], 0), jnp.bfloat16)
    weight = np.where(np.arange(KYW) == 0, 1.0, 2.0)[:, None]
    back_table = jnp.asarray(
        np.concatenate([cosine.T * weight, -sine.T * weight], 0), jnp.bfloat16
    )
    x_table = real_x_table()
    hbm = pl.BlockSpec(memory_space=pl.ANY)
    smem = pl.BlockSpec(memory_space=pltpu.SMEM)
    dma = pltpu.SemaphoreType.DMA
    planes = pl.pallas_call(
        functools.partial(middle_kernel, n_ha, n_gz, depth),
        out_shape=jax.ShapeDtypeStruct((depth, count * GROUP, rows), jnp.bfloat16),
        in_specs=[hbm, hbm, hbm, smem, smem],
        out_specs=pl.BlockSpec(memory_space=pltpu.VMEM),
        scratch_shapes=[
            pltpu.VMEM(velocity.shape, jnp.bfloat16),
            pltpu.VMEM(y_table.shape, jnp.bfloat16),
            pltpu.VMEM(x_table.shape, jnp.bfloat16),
            pltpu.VMEM((n_ha, n_gz, block_rows, rows), jnp.bfloat16),
            pltpu.VMEM((n_ha, n_gz, block_rows, rows), jnp.bfloat16),
            pltpu.VMEM((bulk, NX), jnp.float32),
            pltpu.VMEM((bulk, NX), jnp.float32),
            pltpu.VMEM((bulk, NX), jnp.float32),
            pltpu.VMEM((bulk, NX), jnp.bfloat16),
            pltpu.VMEM((n_ha, n_gz, block_rows, rows), jnp.bfloat16),
            pltpu.VMEM((count, block_rows, rows), jnp.bfloat16),
            pltpu.VMEM((2 * depth, LANES), jnp.float32),
            pltpu.VMEM((n_gz, 2 * depth, LANES), jnp.float32),
            dma((depth + 1,)), dma, dma((2,)),
            dma((count,)), dma((count,)), dma((count,)), dma((count,)),
            dma((n_gz,)), dma((n_gz,)),
        ],
        compiler_params=pltpu.CompilerParams(
            collective_id=0, has_side_effects=True, vmem_limit_bytes=60 * 1024 * 1024
        ),
    )(velocity, y_table, x_table, lower_coef, upper_coef)
    result = jnp.einsum("zkx,ky->zxy", planes, back_table, preferred_element_type=jnp.float32)
    return result.astype(jnp.bfloat16)


def solution(mesh):
    n_ha, n_gz = mesh.shape["ha"], mesh.shape["gz"]
    by_channel = (
        2 * KYW == n_ha * n_gz * GROUP
        and n_ha % 2 == 0
        and NX % (n_ha * LANES) == 0
    )
    body = functools.partial(body_channels, n_ha, n_gz) if by_channel else body_general
    in_specs = (P("gz", "ha", None), P("gz"), P("gz"))
    out_specs = P("gz", "ha", None)
    return jax.shard_map(body, mesh=mesh, in_specs=in_specs, out_specs=out_specs, check_vma=False)
```
